32 devices in a mesh: groups: 2 (over y), rows: 4 (over z), samples: 4 (over x, core).
Axes of the slice: x: 2, y: 2, z: 4, core: 2. Of those that a mesh axis runs over, the one named last changes fastest.
Arguments:
- ancestor: float32 [4096, 512], P(('groups', 'rows'), 'samples'), parts along dimension 0, may hold values from -6 to 6
- panels: float32 [2, 2, 1024, 256], P(None, None, 'rows', 'samples'), may hold values from -0.1875 to 0.1875
- row_map: int32 [2, 1024], P(None, 'rows'), may hold values from 0 to 511
- offsets: int32 [2], replicated, may hold values from 0 to 1536
- noise: float32 [4096, 512], P('groups', 'samples'), parts along dimension 0, may hold values from -6 to 6
- inverse: float32 [2, 2, 256, 256], P(None, None, 'rows'), as said below
- inner_link: float32 [2, 256, 256], P(None, 'rows'), may hold values from -0.375 to 0.375
- cross_link: float32 [2, 2, 256, 256], P(None, None, 'rows'), may hold values from -0.25 to 0.25
Outputs:
- solved: float32 [2, 2, 256, 1024], P(None, None, 'rows', ('groups', 'samples')), parts along dimension 3
The draws below stay inside these ranges and needn't reach their ends.
There are 2 independent parts, one for each index of `groups`. The reference program is written for one: setup_inputs(seed, part) draws one part's arguments, and reference() takes and returns one part's arrays. A program takes and returns all parts, laid end to end along the dimension named above; an argument that names none is the same for every part. Nothing has to cross between parts.
Inputs may be any that keep to these rules, and one draw needn't show every extreme that they name: inverse[p, b] is upper triangular: entry (i, j) is zero for j < i, and its diagonal is positive.
All inputs are finite; a program needn't handle non-finite values.
Results may differ from the reference program's by a relative error of at most 0.0003.
Values sent between devices are 32-bit elements; how exact they have to be, the bound alone decides.
A program may use at most 64 MiB of HBM per device.

```python
import math
import jax
import jax.numpy as jnp
from jax import lax

BLOCK = 256
ROW_DEV = 256
ANC_DEV = 512
NOISE = 2048
PANEL = 512
FRONT = 1024
ANC = 2048
SAMPLES = 512


def draw_inverse(key, part):
    diag_key, upper_key = jax.random.split(jax.random.fold_in(key, 7))
    diagonal = jax.random.uniform(diag_key, (2, 2, BLOCK), jnp.float32, 0.5, 1.5)
    upper = jax.random.normal(upper_key, (2, 2, BLOCK, BLOCK), jnp.float32) / math.sqrt(BLOCK)
    row_ids = jnp.arange(BLOCK)[:, None]
    col_ids = jnp.arange(BLOCK)[None, :]
    above = col_ids > row_ids
    on_diag = (col_ids == row_ids).astype(jnp.float32)
    return jnp.where(above, upper, 0.0) + diagonal[..., None] * on_diag


def place_ends(array, rng, low, top_value):
    extent = array.shape
    spot = [jax.random.randint(jax.random.fold_in(rng, axis), (), 0, extent[axis]) for axis in range(len(extent))]
    array = array.at[tuple(spot)].set(low)
    longest = extent.index(max(extent))
    spot[longest] = (spot[longest] + 1) % extent[longest]
    return array.at[tuple(spot)].set(top_value)


def shard_levels(stream_key, extent, pieces, smallest, high):
    level = 1.0
    for position, shards_of in pieces:
        steps = jax.random.uniform(jax.random.fold_in(jax.random.fold_in(stream_key, 6), position), (shards_of,), jnp.float32, smallest / len(pieces), high / len(pieces))
        level = level * jnp.repeat(jnp.exp(steps), extent[position] // shards_of).reshape((-1,) + (1,) * (len(extent) - 1 - position))
    return level


def gaussian(rng, dims, spread, limit, pieces=(), held_as=jnp.bfloat16):
    drawn = jax.random.normal(rng, dims, jnp.float32) * spread
    if len(pieces) > 0:
        drawn = shard_levels(rng, dims, pieces, -0.22, 0.18) * drawn
    return jnp.clip(drawn, min=-limit, max=limit).astype(held_as)


def setup_inputs(seed: int = 0, part: int = 0) -> dict:
    arg_keys = jax.random.split(jax.random.key(seed), 9)
    part_keys = jax.random.split(jax.random.fold_in(arg_keys[8], part), 9)
    return {
        "ancestor": gaussian(part_keys[0], (ANC, SAMPLES), 1.0, 6.0, ((0, 4), (1, 4)), jnp.float32),
        "panels": gaussian(arg_keys[1], (2, 2, FRONT, BLOCK), FRONT ** -0.5, 0.1875, ((2, 4), (3, 4)), jnp.float32),
        "row_map": place_ends(jax.random.randint(arg_keys[2], (2, FRONT), 0, ANC_DEV), jax.random.fold_in(arg_keys[2], 1), 0, ANC_DEV - 1).astype(jnp.int32),
        "offsets": jax.random.randint(arg_keys[3], (2,), 0, NOISE - PANEL + 1).astype(jnp.int32),
        "noise": gaussian(part_keys[4], (NOISE, SAMPLES), 1.0, 6.0, ((1, 4),), jnp.float32),
        "inverse": draw_inverse(jax.random.fold_in(arg_keys[8], 71), part),
        "inner_link": gaussian(arg_keys[6], (2, BLOCK, BLOCK), BLOCK ** -0.5, 0.375, ((1, 4),), jnp.float32),
        "cross_link": gaussian(arg_keys[7], (2, 2, BLOCK, BLOCK), (2 * BLOCK) ** -0.5, 0.25, ((2, 4),), jnp.float32),
    }


def product(left, right):
    return jnp.dot(left, right, precision=lax.Precision.HIGHEST, preferred_element_type=jnp.float32)


def reference(ancestor, panels, row_map, offsets, noise, inverse, inner_link, cross_link):
    owners = (jnp.arange(FRONT, dtype=jnp.int32) // ROW_DEV) * ANC_DEV
    solved = [[None, None], [None, None]]
    for which_panel in (1, 0):
        indices = (row_map[which_panel] + owners).astype(jnp.int32)
        front_rows = jnp.take(ancestor, indices, axis=0)
        window = lax.dynamic_slice_in_dim(noise, offsets[which_panel], 2 * BLOCK, 0)
        for which_block in (1, 0):
            partial_value = product(panels[which_panel, which_block].T, front_rows)
            if which_block == 0:
                partial_value = partial_value + product(inner_link[which_panel].T, solved[which_panel][1])
            if which_panel == 0:
                for earlier in (0, 1):
                    partial_value = partial_value + product(cross_link[which_block, earlier].T, solved[1][earlier])
            target = window[which_block * BLOCK:(which_block + 1) * BLOCK]
            solved[which_panel][which_block] = product(inverse[which_panel, which_block], target - partial_value)
    return jnp.stack([jnp.stack(solved[0]), jnp.stack(solved[1])])
```

```python
import functools

import jax
import jax.numpy as jnp
from jax import lax
from jax.experimental import pallas as pl
from jax.experimental.pallas import tpu as pltpu
from jax.sharding import PartitionSpec as P

F32 = jnp.float32
BF16 = jnp.bfloat16
NN = ((1,), (0,))
NT = ((1,), (1,))


def product(left, right):
    return jnp.dot(left, right, precision=lax.Precision.HIGHEST, preferred_element_type=F32)


def apply_inverse(target, partial_value, inverse_rows):
    rows_here = inverse_rows.shape[0]
    share = lax.psum_scatter(partial_value, "rows", scatter_dimension=0, tiled=True)
    first_own = lax.axis_index("rows") * rows_here
    residue = lax.dynamic_slice_in_dim(target, first_own, rows_here, 0) - share
    return product(inverse_rows, lax.all_gather(residue, "rows", axis=0, tiled=True))


def plain(ancestor, panels, row_map, offsets, noise, inverse, inner_link, cross_link):
    block_rows = inverse.shape[3]
    solved = [[None, None], [None, None]]
    for p in (1, 0):
        front_rows = jnp.take(ancestor, row_map[p], axis=0)
        window = lax.dynamic_slice_in_dim(noise, offsets[p], 2 * block_rows, 0)
        for b in (1, 0):
            whole = lax.all_gather(panels[p, b], "samples", axis=1, tiled=True)
            partial_value = product(whole.T, front_rows)
            if b == 0:
                partial_value = partial_value + product(inner_link[p].T, solved[p][1])
            if p == 0:
                for e in (0, 1):
                    partial_value = partial_value + product(cross_link[b, e].T, solved[1][e])
            target = window[b * block_rows : (b + 1) * block_rows]
            solved[p][b] = apply_inverse(target, partial_value, inverse[p, b])
    return jnp.stack([jnp.stack(solved[0]), jnp.stack(solved[1])])


def split(a):
    hi = a.astype(BF16)
    return hi, (a - hi.astype(F32)).astype(BF16)


def dot(a, b, dims):
    return lax.dot_general(a, b, (dims, ((), ())), preferred_element_type=F32)


def mm(a, b, dims):
    ah, al = split(a)
    bh, bl = split(b)
    m = a.shape[0]
    both = dot(jnp.concatenate([ah, al], 0), bh, dims)
    return both[:m] + (both[m:] + dot(ah, bl, dims))


def kernel(
    n, rm, off, anc_h, pan_h, noise_h, inv_h, lnk_h, crs_h, out,
    anc, pan, nz, mats, pk, fr, tt, rsend, rrecv, osend, orecv,
    loc, ps, pr, zs, zr, b1s, b1r, b2s, b2r, b3s, b3r, rss, rsr, oss, osr,
):
    y = lax.axis_index("groups")
    z = lax.axis_index("rows")
    s = lax.axis_index("samples")
    x, c = s // 2, s % 2
    sx = (s + 2) % 4
    sib = s + 1 - 2 * c
    sxsib = (sib + 2) % 4
    to_x, to_y, to_c = {"samples": sx}, {"groups": 1 - y}, {"samples": sib}
    block = mats.shape[3]
    share = mats.shape[2]
    piece = share // 8
    half = mats.shape[0] // 2
    cols = pan.shape[3]
    w = rsend.shape[2]

    def remote(src, dst, ss, rs, where):
        return pltpu.make_async_remote_copy(
            src_ref=src, dst_ref=dst, send_sem=ss, recv_sem=rs,
            device_id=where, device_id_type=pl.DeviceIdType.MESH,
        )

    local = [
        pltpu.make_async_copy(pan_h, pan, loc.at[0]),
        pltpu.make_async_copy(inv_h, mats.at[0:4, z], loc.at[1]),
        pltpu.make_async_copy(lnk_h, mats.at[4:6, z], loc.at[2]),
        pltpu.make_async_copy(crs_h, mats.at[6:10, z], loc.at[3]),
        pltpu.make_async_copy(anc_h, anc, loc.at[4]),
        pltpu.make_async_copy(noise_h, nz, loc.at[5]),
    ]
    for copy in local:
        copy.start()

    barrier = pltpu.get_barrier_semaphore()
    peers = [{"rows": (z + k) % n} for k in range(1, n)] + [to_x, to_y, to_c]
    for peer in peers:
        pl.semaphore_signal(barrier, inc=1, device_id=peer, device_id_type=pl.DeviceIdType.MESH)

    local[0].wait()
    for p in range(2):
        pk[s, p] = jnp.concatenate([pan[p, 0], pan[p, 1]], axis=1)

    pl.semaphore_wait(barrier, len(peers))

    pending = []

    def go(copy):
        copy.start()
        pending.append(copy)
        return copy

    pan_x = go(remote(pk.at[s], pk.at[s], ps.at[0], pr.at[0], to_x))
    pan_c = go(remote(pk.at[s], pk.at[s], ps.at[1], pr.at[1], to_c))
    for i in (1, 2, 3):
        local[i].wait()

    def at_rows(q):
        return pl.ds(pl.multiple_of(q * piece, piece), piece)

    q = c * 4 + x * 2 + y
    qx = c * 4 + (1 - x) * 2 + y
    qy = c * 4 + x * 2 + (1 - y)
    sets = [(0, half), (half, 2 * half)]
    stage_z = {}
    for k in range(1, n):
        for g, (lo, hi) in enumerate(sets):
            ref = mats.at[lo:hi, z, at_rows(q)]
            stage_z[k, g] = go(remote(ref, ref, zs.at[k, g], zr.at[k, g], {"rows": (z + k) % n}))

    local[4].wait()
    for p in (1, 0):
        def rows8(i, carry, p=p):
            for r in range(8):
                fr[p, pl.ds(i * 8 + r, 1), :] = anc[pl.ds(rm[p, i * 8 + r], 1), :]
            return carry

        lax.fori_loop(0, fr.shape[1] // 8, rows8, 0)
    local[5].wait()
    for p in range(2):
        tt[p] = nz[pl.ds(off[p], 2 * block), :].T

    pan_x.wait_recv()
    pan_r = go(remote(pk.at[sx], pk.at[sx], ps.at[2], pr.at[2], to_c))

    stage_1 = {}
    for k in range(1, n):
        zz = (z + n - k) % n
        for g, (lo, hi) in enumerate(sets):
            stage_z[k, g].wait_recv()
            ref = mats.at[lo:hi, zz, at_rows(q)]
            stage_1[k, g] = go(remote(ref, ref, b1s.at[k, g], b1r.at[k, g], (to_x, to_y)[g]))

    pan_c.wait_recv()
    pan_r.wait_recv()
    for p in (1, 0):
        ft = fr[p].T
        parts = [mm(ft, pk[i, p], NN) for i in range(4)]
        whole = jnp.concatenate(
            [parts[i][:, b * cols : (b + 1) * cols] for b in range(2) for i in range(4)], axis=1
        )
        for j in range(n):
            rsend[j, p] = whole[j * w : (j + 1) * w]
        for k in range(1, n):
            go(remote(rsend.at[(z + k) % n, p], rrecv.at[k, p], rss.at[k, p], rsr.at[k, p], {"rows": (z + k) % n}))

    stage_2 = {}
    for k in range(1, n):
        zz = (z + n - k) % n
        for g, (lo, hi) in enumerate(sets):
            stage_1[k, g].wait_recv()
            for h, qq in enumerate((q, (qx, qy)[g])):
                ref = mats.at[lo:hi, zz, at_rows(qq)]
                stage_2[k, g, h] = go(remote(ref, ref, b2s.at[k, g, h], b2r.at[k, g, h], (to_y, to_x)[g]))
    stage_3 = {}
    for k in range(1, n):
        zz = (z + n - k) % n
        for g, (lo, hi) in enumerate(sets):
            stage_2[k, g, 0].wait_recv()
            stage_2[k, g, 1].wait_recv()
            ref = mats.at[lo:hi, zz, pl.ds(pl.multiple_of(c * 4 * piece, 4 * piece), 4 * piece)]
            stage_3[k, g] = go(remote(ref, ref, b3s.at[k, g], b3r.at[k, g], to_c))
    for k in range(1, n):
        for g in range(2):
            stage_3[k, g].wait_recv()

    def matrix(i):
        return mats[i].reshape(block, block)

    def residue(p):
        total = rsend[z, p]
        for k in range(1, n):
            remote(rsend.at[(z + k) % n, p], rrecv.at[k, p], rss.at[k, p], rsr.at[k, p], {"rows": (z + k) % n}).wait_recv()
            total = total + rrecv[k, p]
        return tt[p, pl.ds(pl.multiple_of(z * w, w), w), :] - total

    def back(p, first, second):
        for i in range(n):
            cut = slice(i * share, (i + 1) * share)
            osend[p, i] = jnp.concatenate([first[:, cut], second[:, cut]], axis=1)
        orecv[p, z] = osend[p, z]
        for k in range(1, n):
            go(remote(osend.at[p, (z + k) % n], orecv.at[p, z], oss.at[k, p], osr.at[k, p], {"rows": (z + k) % n}))

    res = residue(1)
    s11 = mm(res[:, block:], matrix(3), NT)
    s10 = mm(res[:, :block] - mm(s11, matrix(5), NN), matrix(2), NT)
    back(1, s10, s11)
    res = residue(0)
    s01 = mm(res[:, block:] - mm(s10, matrix(8), NN) - mm(s11, matrix(9), NN), matrix(1), NT)
    s00 = mm(
        res[:, :block] - mm(s10, matrix(6), NN) - mm(s11, matrix(7), NN) - mm(s01, matrix(4), NN),
        matrix(0), NT,
    )
    back(0, s00, s01)

    for p in (1, 0):
        for k in range(1, n):
            src = (z + n - k) % n
            remote(osend.at[p, src], orecv.at[p, src], oss.at[k, p], osr.at[k, p], {"rows": src}).wait_recv()
        out[p] = orecv[p].reshape(n * w, 2 * share).T.reshape(2, share, n * w)

    for copy in pending:
        copy.wait_send()


def fused(n, ancestor, panels, row_map, offsets, noise, inverse, inner_link, cross_link):
    share, block = inverse.shape[2:]
    lanes = ancestor.shape[1]
    w = lanes // n
    dma = pltpu.SemaphoreType.DMA
    anyspace = pl.BlockSpec(memory_space=pl.ANY)
    smem = pl.BlockSpec(memory_space=pltpu.SMEM)
    return pl.pallas_call(
        functools.partial(kernel, n),
        name="substitute",
        out_shape=jax.ShapeDtypeStruct((2, 2, share, lanes), F32),
        in_specs=[smem, smem] + [anyspace] * 6,
        out_specs=pl.BlockSpec(memory_space=pltpu.VMEM),
        scratch_shapes=[
            pltpu.VMEM(ancestor.shape, F32),
            pltpu.VMEM(panels.shape, F32),
            pltpu.VMEM(noise.shape, F32),
            pltpu.VMEM((10, n, share, block), F32),
            pltpu.VMEM((4, 2, panels.shape[2], 2 * panels.shape[3]), F32),
            pltpu.VMEM((2, row_map.shape[1], lanes), F32),
            pltpu.VMEM((2, lanes, 2 * block), F32),
            pltpu.VMEM((n, 2, w, 2 * block), F32),
            pltpu.VMEM((n, 2, w, 2 * block), F32),
            pltpu.VMEM((2, n, w, 2 * share), F32),
            pltpu.VMEM((2, n, w, 2 * share), F32),
            dma((6,)), dma((3,)), dma((3,)),
            dma((n, 2)), dma((n, 2)),
            dma((n, 2)), dma((n, 2)),
            dma((n, 2, 2)), dma((n, 2, 2)),
            dma((n, 2)), dma((n, 2)),
            dma((n, 2)), dma((n, 2)),
            dma((n, 2)), dma((n, 2)),
        ],
        compiler_params=pltpu.CompilerParams(
            collective_id=0, has_side_effects=True, vmem_limit_bytes=40 * 1024 * 1024
        ),
    )(
        row_map, offsets, ancestor, panels, noise,
        inverse.reshape(4, share, block), inner_link, cross_link.reshape(4, share, block),
    )


def solution(mesh):
    placed = (
        P(("groups", "rows"), "samples"),
        P(None, None, "rows", "samples"),
        P(None, "rows"),
        P(),
        P("groups", "samples"),
        P(None, None, "rows", None),
        P(None, "rows", None),
        P(None, None, "rows", None),
    )
    n = mesh.shape["rows"]

    def local(ancestor, panels, row_map, offsets, noise, inverse, inner_link, cross_link):
        args = (ancestor, panels, row_map, offsets, noise, inverse, inner_link, cross_link)
        fits = (
            mesh.shape["groups"] == 2
            and mesh.shape["samples"] == 4
            and ancestor.shape[1] % (8 * n) == 0
            and inverse.shape[2] % 64 == 0
            and row_map.shape[1] % 8 == 0
        )
        return fused(n, *args) if fits else plain(*args)

    return jax.shard_map(
        local,
        mesh=mesh,
        in_specs=placed,
        out_specs=P(None, None, "rows", ("groups", "samples")),
        check_vma=False,
    )
```

```python
import functools

import jax
import jax.numpy as jnp
from jax import lax
from jax.experimental import pallas as pl
from jax.experimental.pallas import tpu as pltpu
from jax.sharding import PartitionSpec as P

F32 = jnp.float32
BF16 = jnp.bfloat16
NN = ((1,), (0,))
NT = ((1,), (1,))


def product(left, right):
    return jnp.dot(left, right, precision=lax.Precision.HIGHEST, preferred_element_type=F32)


def apply_inverse(target, partial_value, inverse_rows):
    rows_here = inverse_rows.shape[0]
    share = lax.psum_scatter(partial_value, "rows", scatter_dimension=0, tiled=True)
    first_own = lax.axis_index("rows") * rows_here
    residue = lax.dynamic_slice_in_dim(target, first_own, rows_here, 0) - share
    return product(inverse_rows, lax.all_gather(residue, "rows", axis=0, tiled=True))


def plain(ancestor, panels, row_map, offsets, noise, inverse, inner_link, cross_link):
    block_rows = inverse.shape[3]
    solved = [[None, None], [None, None]]
    for p in (1, 0):
        front_rows = jnp.take(ancestor, row_map[p], axis=0)
        window = lax.dynamic_slice_in_dim(noise, offsets[p], 2 * block_rows, 0)
        for b in (1, 0):
            whole = lax.all_gather(panels[p, b], "samples", axis=1, tiled=True)
            partial_value = product(whole.T, front_rows)
            if b == 0:
                partial_value = partial_value + product(inner_link[p].T, solved[p][1])
            if p == 0:
                for e in (0, 1):
                    partial_value = partial_value + product(cross_link[b, e].T, solved[1][e])
            target = window[b * block_rows : (b + 1) * block_rows]
            solved[p][b] = apply_inverse(target, partial_value, inverse[p, b])
    return jnp.stack([jnp.stack(solved[0]), jnp.stack(solved[1])])


def split(a):
    hi = a.astype(BF16)
    return hi, (a - hi.astype(F32)).astype(BF16)


def dot(a, b, dims):
    return lax.dot_general(a, b, (dims, ((), ())), preferred_element_type=F32)


def mm(a, b, dims):
    ah, al = split(a)
    bh, bl = b
    m = a.shape[0]
    both = dot(jnp.concatenate([ah, al], 0), bh, dims)
    return both[:m] + (both[m:] + dot(ah, bl, dims))


def kernel(
    n, rm_h, off_h, anc_h, pan_h, noise_h, inv_h, lnk_h, crs_h, out,
    rm, off, anc, nz, mats, mhi, mlo, pk, fr, tt, rsend, rrecv, osend, orecv,
    loc, ps, pr, zs, zr, b1s, b1r, b2s, b2r, b3s, b3r, rss, rsr, oss, osr,
):
    y = lax.axis_index("groups")
    z = lax.axis_index("rows")
    s = lax.axis_index("samples")
    x, c = s // 2, s % 2
    sx = (s + 2) % 4
    sib = s + 1 - 2 * c
    to_x, to_y, to_c = {"samples": sx}, {"groups": 1 - y}, {"samples": sib}
    block = mats.shape[3]
    share = mats.shape[2]
    piece = share // 8
    half = mats.shape[0] // 2
    w = rsend.shape[2]

    def remote(src, dst, ss, rs, where):
        return pltpu.make_async_remote_copy(
            src_ref=src, dst_ref=dst, send_sem=ss, recv_sem=rs,
            device_id=where, device_id_type=pl.DeviceIdType.MESH,
        )

    local = [
        pltpu.make_async_copy(pan_h.at[1], pk.at[1, :, s], loc.at[0]),
        pltpu.make_async_copy(pan_h.at[0], pk.at[0, :, s], loc.at[1]),
        pltpu.make_async_copy(inv_h, mats.at[0:4, z], loc.at[2]),
        pltpu.make_async_copy(lnk_h, mats.at[4:6, z], loc.at[3]),
        pltpu.make_async_copy(crs_h, mats.at[6:10, z], loc.at[4]),
        pltpu.make_async_copy(rm_h, rm, loc.at[5]),
        pltpu.make_async_copy(off_h, off, loc.at[6]),
        pltpu.make_async_copy(anc_h, anc, loc.at[7]),
        pltpu.make_async_copy(noise_h, nz, loc.at[8]),
    ]
    for copy in local:
        copy.start()

    barrier = pltpu.get_barrier_semaphore()
    peers = [{"rows": (z + k) % n} for k in range(1, n)] + [to_x, to_y, to_c]
    for peer in peers:
        pl.semaphore_signal(barrier, inc=1, device_id=peer, device_id_type=pl.DeviceIdType.MESH)

    for i in range(7):
        local[i].wait()

    pl.semaphore_wait(barrier, len(peers))

    pending = []

    def go(copy):
        copy.start()
        pending.append(copy)
        return copy

    pan_x, pan_c, pan_r = {}, {}, {}
    for p in (1, 0):
        ref = pk.at[p, :, s]
        pan_x[p] = go(remote(ref, ref, ps.at[p, 0], pr.at[p, 0], to_x))
        pan_c[p] = go(remote(ref, ref, ps.at[p, 1], pr.at[p, 1], to_c))

    def at_rows(q):
        return pl.ds(pl.multiple_of(q * piece, piece), piece)

    q = c * 4 + x * 2 + y
    qx = c * 4 + (1 - x) * 2 + y
    qy = c * 4 + x * 2 + (1 - y)
    sets = [(0, half), (half, 2 * half)]
    stage_z = {}
    for k in range(1, n):
        for g, (lo, hi) in enumerate(sets):
            ref = mats.at[lo:hi, z, at_rows(q)]
            stage_z[k, g] = go(remote(ref, ref, zs.at[k, g], zr.at[k, g], {"rows": (z + k) % n}))

    local[7].wait()
    for p in (1, 0):
        def rows8(i, carry, p=p):
            for r in range(8):
                fr[p, pl.ds(i * 8 + r, 1), :] = anc[pl.ds(rm[p, i * 8 + r], 1), :]
            return carry

        lax.fori_loop(0, fr.shape[1] // 8, rows8, 0)
    local[8].wait()
    for p in range(2):
        tt[p] = nz[pl.ds(off[p], 2 * block), :].T

    stage_1 = {}

    def forward(p):
        pan_x[p].wait_recv()
        ref = pk.at[p, :, sx]
        pan_r[p] = go(remote(ref, ref, ps.at[p, 2], pr.at[p, 2], to_c))

    def reduce(p):
        ft = fr[p].T
        pan_c[p].wait_recv()
        pan_r[p].wait_recv()
        whole = jnp.concatenate(
            [mm(ft, split(pk[p, b].reshape(block, ft.shape[1])), NT) for b in range(2)], axis=1
        )
        for j in range(n):
            rsend[j, p] = whole[j * w : (j + 1) * w]
        for k in range(1, n):
            go(remote(rsend.at[(z + k) % n, p], rrecv.at[k, p], rss.at[k, p], rsr.at[k, p], {"rows": (z + k) % n}))

    forward(1)
    reduce(1)
    forward(0)
    for k in range(1, n):
        zz = (z + n - k) % n
        for g, (lo, hi) in enumerate(sets):
            stage_z[k, g].wait_recv()
            ref = mats.at[lo:hi, zz, at_rows(q)]
            stage_1[k, g] = go(remote(ref, ref, b1s.at[k, g], b1r.at[k, g], (to_x, to_y)[g]))
    reduce(0)

    stage_2 = {}
    for k in range(1, n):
        zz = (z + n - k) % n
        for g, (lo, hi) in enumerate(sets):
            stage_1[k, g].wait_recv()
            for h, qq in enumerate((q, (qx, qy)[g])):
                ref = mats.at[lo:hi, zz, at_rows(qq)]
                stage_2[k, g, h] = go(remote(ref, ref, b2s.at[k, g, h], b2r.at[k, g, h], (to_y, to_x)[g]))
    stage_3 = {}
    for k in range(1, n):
        zz = (z + n - k) % n
        for g, (lo, hi) in enumerate(sets):
            stage_2[k, g, 0].wait_recv()
            stage_2[k, g, 1].wait_recv()
            ref = mats.at[lo:hi, zz, pl.ds(pl.multiple_of(c * 4 * piece, 4 * piece), 4 * piece)]
            stage_3[k, g] = go(remote(ref, ref, b3s.at[k, g], b3r.at[k, g], to_c))
    for k in range(1, n):
        for g in range(2):
            stage_3[k, g].wait_recv()

    for i in range(2 * half):
        mhi[i], mlo[i] = split(mats[i].reshape(block, block))

    def matrix(i):
        return mhi[i], mlo[i]

    def residue(p):
        total = rsend[z, p]
        for k in range(1, n):
            remote(rsend.at[(z + k) % n, p], rrecv.at[k, p], rss.at[k, p], rsr.at[k, p], {"rows": (z + k) % n}).wait_recv()
            total = total + rrecv[k, p]
        return tt[p, pl.ds(pl.multiple_of(z * w, w), w), :] - total

    def back(p, first, second):
        for i in range(n):
            cut = slice(i * share, (i + 1) * share)
            osend[p, i] = jnp.concatenate([first[:, cut], second[:, cut]], axis=1)
        orecv[p, z] = osend[p, z]
        for k in range(1, n):
            go(remote(osend.at[p, (z + k) % n], orecv.at[p, z], oss.at[k, p], osr.at[k, p], {"rows": (z + k) % n}))

    res = residue(1)
    s11 = mm(res[:, block:], matrix(3), NT)
    s10 = mm(res[:, :block] - mm(s11, matrix(5), NN), matrix(2), NT)
    back(1, s10, s11)
    res = residue(0)
    s01 = mm(res[:, block:] - mm(s10, matrix(8), NN) - mm(s11, matrix(9), NN), matrix(1), NT)
    s00 = mm(
        res[:, :block] - mm(s10, matrix(6), NN) - mm(s11, matrix(7), NN) - mm(s01, matrix(4), NN),
        matrix(0), NT,
    )
    back(0, s00, s01)

    for p in (1, 0):
        for k in range(1, n):
            src = (z + n - k) % n
            remote(osend.at[p, src], orecv.at[p, src], oss.at[k, p], osr.at[k, p], {"rows": src}).wait_recv()
        out[p] = orecv[p].reshape(n * w, 2 * share).T.reshape(2, share, n * w)

    for copy in pending:
        copy.wait_send()


def fused(n, ancestor, panels, row_map, offsets, noise, inverse, inner_link, cross_link):
    share, block = inverse.shape[2:]
    lanes = ancestor.shape[1]
    w = lanes // n
    dma = pltpu.SemaphoreType.DMA
    anyspace = pl.BlockSpec(memory_space=pl.ANY)
    return pl.pallas_call(
        functools.partial(kernel, n),
        name="substitute",
        out_shape=jax.ShapeDtypeStruct((2, 2, share, lanes), F32),
        in_specs=[anyspace] * 8,
        out_specs=pl.BlockSpec(memory_space=pltpu.VMEM),
        scratch_shapes=[
            pltpu.SMEM(row_map.shape, jnp.int32),
            pltpu.SMEM(offsets.shape, jnp.int32),
            pltpu.VMEM(ancestor.shape, F32),
            pltpu.VMEM(noise.shape, F32),
            pltpu.VMEM((10, n, share, block), F32),
            pltpu.VMEM((10, block, block), BF16),
            pltpu.VMEM((10, block, block), BF16),
            pltpu.VMEM((2, 2, 4, panels.shape[3], panels.shape[2]), F32),
            pltpu.VMEM((2, row_map.shape[1], lanes), F32),
            pltpu.VMEM((2, lanes, 2 * block), F32),
            pltpu.VMEM((n, 2, w, 2 * block), F32),
            pltpu.VMEM((n, 2, w, 2 * block), F32),
            pltpu.VMEM((2, n, w, 2 * share), F32),
            pltpu.VMEM((2, n, w, 2 * share), F32),
            dma((9,)), dma((2, 3)), dma((2, 3)),
            dma((n, 2)), dma((n, 2)),
            dma((n, 2)), dma((n, 2)),
            dma((n, 2, 2)), dma((n, 2, 2)),
            dma((n, 2)), dma((n, 2)),
            dma((n, 2)), dma((n, 2)),
            dma((n, 2)), dma((n, 2)),
        ],
        compiler_params=pltpu.CompilerParams(collective_id=0, has_side_effects=True),
    )(
        row_map, offsets, ancestor, panels.swapaxes(2, 3), noise,
        inverse.reshape(4, share, block), inner_link, cross_link.reshape(4, share, block),
    )


def solution(mesh):
    placed = (
        P(("groups", "rows"), "samples"),
        P(None, None, "rows", "samples"),
        P(None, "rows"),
        P(),
        P("groups", "samples"),
        P(None, None, "rows", None),
        P(None, "rows", None),
        P(None, None, "rows", None),
    )
    n = mesh.shape["rows"]

    def local(ancestor, panels, row_map, offsets, noise, inverse, inner_link, cross_link):
        args = (ancestor, panels, row_map, offsets, noise, inverse, inner_link, cross_link)
        fits = (
            mesh.shape["groups"] == 2
            and mesh.shape["samples"] == 4
            and ancestor.shape[1] % (8 * n) == 0
            and inverse.shape[2] % 64 == 0
            and row_map.shape[1] % 8 == 0
        )
        return fused(n, *args) if fits else plain(*args)

    return jax.shard_map(
        local,
        mesh=mesh,
        in_specs=placed,
        out_specs=P(None, None, "rows", ("groups", "samples")),
        check_vma=False,
    )
```

```python
import functools

import jax
import jax.numpy as jnp
from jax import lax
from jax.experimental import pallas as pl
from jax.experimental.pallas import tpu as pltpu
from jax.sharding import PartitionSpec as P

F32 = jnp.float32
BF16 = jnp.bfloat16
NN = ((1,), (0,))
NT = ((1,), (1,))


def product(left, right):
    return jnp.dot(left, right, precision=lax.Precision.HIGHEST, preferred_element_type=F32)


def apply_inverse(target, partial_value, inverse_rows):
    rows_here = inverse_rows.shape[0]
    share = lax.psum_scatter(partial_value, "rows", scatter_dimension=0, tiled=True)
    first_own = lax.axis_index("rows") * rows_here
    residue = lax.dynamic_slice_in_dim(target, first_own, rows_here, 0) - share
    return product(inverse_rows, lax.all_gather(residue, "rows", axis=0, tiled=True))


def plain(ancestor, panels, row_map, offsets, noise, inverse, inner_link, cross_link):
    block_rows = inverse.shape[3]
    solved = [[None, None], [None, None]]
    for p in (1, 0):
        front_rows = jnp.take(ancestor, row_map[p], axis=0)
        window = lax.dynamic_slice_in_dim(noise, offsets[p], 2 * block_rows, 0)
        for b in (1, 0):
            whole = lax.all_gather(panels[p, b], "samples", axis=1, tiled=True)
            partial_value = product(whole.T, front_rows)
            if b == 0:
                partial_value = partial_value + product(inner_link[p].T, solved[p][1])
            if p == 0:
                for e in (0, 1):
                    partial_value = partial_value + product(cross_link[b, e].T, solved[1][e])
            target = window[b * block_rows : (b + 1) * block_rows]
            solved[p][b] = apply_inverse(target, partial_value, inverse[p, b])
    return jnp.stack([jnp.stack(solved[0]), jnp.stack(solved[1])])


def split(a):
    hi = a.astype(BF16)
    return hi, (a - hi.astype(F32)).astype(BF16)


def dot(a, b, dims):
    return lax.dot_general(a, b, (dims, ((), ())), preferred_element_type=F32)


def pre(a, b, dims=NT):
    ah, al = a
    bh, bl = b
    return dot(ah, bh, dims) + (dot(al, bh, dims) + dot(ah, bl, dims))


def mm(a, b, dims):
    ah, al = split(a)
    bh, bl = b
    m = a.shape[0]
    both = dot(jnp.concatenate([ah, al], 0), bh, dims)
    return both[:m] + (both[m:] + dot(ah, bl, dims))


def kernel(
    n, rm_h, off_h, anc_h, pan_h, noise_h, inv_h, lnk_h, crs_h, out,
    rm, off, anc, nz, mats, mhi, mlo, pk, fr, tt, rsend, rone, rsum, rtwo, osend, orecv,
    loc, ps, pr, zs, zr, b1s, b1r, b2s, b2r, b3s, b3r, r1s, r1r, r2s, r2r, oss, osr,
):
    y = lax.axis_index("groups")
    z = lax.axis_index("rows")
    s = lax.axis_index("samples")
    x, c = s // 2, s % 2
    sx = (s + 2) % 4
    sib = s + 1 - 2 * c
    to_x, to_y, to_c = {"samples": sx}, {"groups": 1 - y}, {"samples": sib}
    block = mats.shape[3]
    share = mats.shape[2]
    piece = share // 8
    w = rsend.shape[3]
    order = ((1, 1), (1, 0), (0, 1), (0, 0))
    odd, high = z % 2, z // 2
    to_1, to_2 = {"rows": z + 1 - 2 * odd}, {"rows": (z + 2) % 4}

    def remote(src, dst, ss, rs, where):
        return pltpu.make_async_remote_copy(
            src_ref=src, dst_ref=dst, send_sem=ss, recv_sem=rs,
            device_id=where, device_id_type=pl.DeviceIdType.MESH,
        )

    local = [
        pltpu.make_async_copy(pan_h.at[p, b], pk.at[p, b, s], loc.at[i]) for i, (p, b) in enumerate(order)
    ] + [
        pltpu.make_async_copy(inv_h, mats.at[0:4, z], loc.at[4]),
        pltpu.make_async_copy(lnk_h, mats.at[4:6, z], loc.at[5]),
        pltpu.make_async_copy(crs_h, mats.at[6:10, z], loc.at[6]),
        pltpu.make_async_copy(rm_h, rm, loc.at[7]),
        pltpu.make_async_copy(off_h, off, loc.at[8]),
        pltpu.make_async_copy(anc_h, anc, loc.at[9]),
        pltpu.make_async_copy(noise_h, nz, loc.at[10]),
    ]
    for copy in local:
        copy.start()

    barrier = pltpu.get_barrier_semaphore()
    peers = [{"rows": (z + k) % n} for k in range(1, n)] + [to_x, to_y, to_c]
    for peer in peers:
        pl.semaphore_signal(barrier, inc=1, device_id=peer, device_id_type=pl.DeviceIdType.MESH)

    for i in range(9):
        local[i].wait()

    pl.semaphore_wait(barrier, len(peers))

    pending = []

    def go(copy):
        copy.start()
        pending.append(copy)
        return copy

    pan_x, pan_c, pan_r = {}, {}, {}
    for i, (p, b) in enumerate(order):
        ref = pk.at[p, b, s]
        pan_x[i] = go(remote(ref, ref, ps.at[i, 0], pr.at[i, 0], to_x))
        pan_c[i] = go(remote(ref, ref, ps.at[i, 1], pr.at[i, 1], to_c))

    def at_rows(q):
        return pl.ds(pl.multiple_of(q * piece, piece), piece)

    q = c * 4 + x * 2 + y
    qx = c * 4 + (1 - x) * 2 + y
    qy = c * 4 + x * 2 + (1 - y)
    sets = [(0, 7), (7, 10)]
    stage_z = {}
    for k in range(1, n):
        for g, (lo, hi) in enumerate(sets):
            ref = mats.at[lo:hi, z, at_rows(q)]
            stage_z[k, g] = go(remote(ref, ref, zs.at[k, g], zr.at[k, g], {"rows": (z + k) % n}))

    local[9].wait()
    for p in (1, 0):
        def rows8(i, carry, p=p):
            for r in range(8):
                fr[p, pl.ds(i * 8 + r, 1), :] = anc[pl.ds(rm[p, i * 8 + r], 1), :]
            return carry

        lax.fori_loop(0, fr.shape[1] // 8, rows8, 0)
    front = [split(fr[p].T) for p in range(2)]
    stage_1, stage_2, stage_3, step_1, step_2 = {}, {}, {}, {}, {}

    def forward(i):
        p, b = order[i]
        pan_x[i].wait_recv()
        ref = pk.at[p, b, sx]
        pan_r[i] = go(remote(ref, ref, ps.at[i, 2], pr.at[i, 2], to_c))

    def reduce_1(i):
        p, b = order[i]
        pan_c[i].wait_recv()
        pan_r[i].wait_recv()
        whole = pre(front[p], split(pk[p, b].reshape(block, fr.shape[1])))
        for j in range(n):
            rsend[i, j % 2, j // 2] = whole[j * w : (j + 1) * w]
        step_1[i] = go(remote(rsend.at[i, 1 - odd], rone.at[i], r1s.at[i], r1r.at[i], to_1))

    def reduce_2(i):
        step_1[i].wait_recv()
        rsum[i] = rsend[i, odd, 1 - high] + rone[i, 1 - high]
        step_2[i] = go(remote(rsum.at[i], rtwo.at[i], r2s.at[i], r2r.at[i], to_2))

    def mats_1(k):
        zz = (z + n - k) % n
        for g, (lo, hi) in enumerate(sets):
            stage_z[k, g].wait_recv()
            ref = mats.at[lo:hi, zz, at_rows(q)]
            stage_1[k, g] = go(remote(ref, ref, b1s.at[k, g], b1r.at[k, g], (to_x, to_y)[g]))
            stage_2[k, g, 0] = go(remote(ref, ref, b2s.at[k, g, 0], b2r.at[k, g, 0], (to_y, to_x)[g]))

    def mats_2(k):
        zz = (z + n - k) % n
        for g, (lo, hi) in enumerate(sets):
            stage_1[k, g].wait_recv()
            ref = mats.at[lo:hi, zz, at_rows((qx, qy)[g])]
            stage_2[k, g, 1] = go(remote(ref, ref, b2s.at[k, g, 1], b2r.at[k, g, 1], (to_y, to_x)[g]))

    def mats_3(k):
        zz = (z + n - k) % n
        for g, (lo, hi) in enumerate(sets):
            stage_2[k, g, 0].wait_recv()
            stage_2[k, g, 1].wait_recv()
            ref = mats.at[lo:hi, zz, pl.ds(pl.multiple_of(c * 4 * piece, 4 * piece), 4 * piece)]
            stage_3[k, g] = go(remote(ref, ref, b3s.at[k, g], b3r.at[k, g], to_c))

    forward(0)
    reduce_1(0)
    forward(1)
    reduce_1(1)
    mats_1(1)
    forward(2)
    reduce_1(2)
    reduce_2(0)
    forward(3)
    reduce_1(3)
    mats_1(2)
    reduce_2(1)
    mats_2(1)
    mats_1(3)
    reduce_2(2)
    mats_2(2)
    mats_3(1)
    reduce_2(3)
    mats_2(3)
    mats_3(2)
    local[10].wait()
    for p in range(2):
        tt[p] = nz[pl.ds(off[p], 2 * block), :].T
    mats_3(3)
    for k in range(1, n):
        for g in range(2):
            stage_3[k, g].wait_recv()

    for i in range(mats.shape[0]):
        mhi[i], mlo[i] = split(mats[i].reshape(block, block))

    def matrix(i):
        return mhi[i], mlo[i]

    def residue(i):
        p, b = order[i]
        step_2[i].wait_recv()
        total = rsend[i, odd, high] + rone[i, high] + rtwo[i]
        return tt[p, pl.ds(pl.multiple_of(z * w, w), w), b * block : (b + 1) * block] - total

    def back(p, first, second):
        for i in range(n):
            cut = slice(i * share, (i + 1) * share)
            osend[p, i] = jnp.concatenate([first[:, cut], second[:, cut]], axis=1)
        orecv[p, z] = osend[p, z]
        for k in range(1, n):
            go(remote(osend.at[p, (z + k) % n], orecv.at[p, z], oss.at[k, p], osr.at[k, p], {"rows": (z + k) % n}))

    s11 = mm(residue(0), matrix(3), NT)
    s10 = mm(residue(1) - mm(s11, matrix(5), NN), matrix(2), NT)
    back(1, s10, s11)
    s01 = mm(residue(2) - mm(s10, matrix(8), NN) - mm(s11, matrix(9), NN), matrix(1), NT)
    s00 = mm(
        residue(3) - mm(s10, matrix(6), NN) - mm(s11, matrix(7), NN) - mm(s01, matrix(4), NN),
        matrix(0), NT,
    )
    back(0, s00, s01)

    for p in (1, 0):
        for k in range(1, n):
            src = (z + n - k) % n
            remote(osend.at[p, src], orecv.at[p, src], oss.at[k, p], osr.at[k, p], {"rows": src}).wait_recv()
        out[p] = orecv[p].reshape(n * w, 2 * share).T.reshape(2, share, n * w)

    for copy in pending:
        copy.wait_send()


def fused(n, ancestor, panels, row_map, offsets, noise, inverse, inner_link, cross_link):
    share, block = inverse.shape[2:]
    lanes = ancestor.shape[1]
    w = lanes // n
    dma = pltpu.SemaphoreType.DMA
    anyspace = pl.BlockSpec(memory_space=pl.ANY)
    return pl.pallas_call(
        functools.partial(kernel, n),
        name="substitute",
        out_shape=pltpu.VMEM((2, 2, share, lanes), F32),
        in_specs=[anyspace] * 8,
        out_specs=pl.BlockSpec(memory_space=pltpu.VMEM),
        scratch_shapes=[
            pltpu.SMEM(row_map.shape, jnp.int32),
            pltpu.SMEM(offsets.shape, jnp.int32),
            pltpu.VMEM(ancestor.shape, F32),
            pltpu.VMEM(noise.shape, F32),
            pltpu.VMEM((10, n, share, block), F32),
            pltpu.VMEM((10, block, block), BF16),
            pltpu.VMEM((10, block, block), BF16),
            pltpu.VMEM((2, 2, 4, panels.shape[3], panels.shape[2]), F32),
            pltpu.VMEM((2, row_map.shape[1], lanes), F32),
            pltpu.VMEM((2, lanes, 2 * block), F32),
            pltpu.VMEM((4, 2, 2, w, block), F32),
            pltpu.VMEM((4, 2, w, block), F32),
            pltpu.VMEM((4, w, block), F32),
            pltpu.VMEM((4, w, block), F32),
            pltpu.VMEM((2, n, w, 2 * share), F32),
            pltpu.VMEM((2, n, w, 2 * share), F32),
            dma((11,)), dma((4, 3)), dma((4, 3)),
            dma((n, 2)), dma((n, 2)),
            dma((n, 2)), dma((n, 2)),
            dma((n, 2, 2)), dma((n, 2, 2)),
            dma((n, 2)), dma((n, 2)),
            dma((4,)), dma((4,)),
            dma((4,)), dma((4,)),
            dma((n, 2)), dma((n, 2)),
        ],
        compiler_params=pltpu.CompilerParams(collective_id=0, has_side_effects=True),
    )(
        row_map, offsets, ancestor, panels.swapaxes(2, 3), noise,
        inverse.reshape(4, share, block), inner_link, cross_link.reshape(4, share, block),
    )


def solution(mesh):
    placed = (
        P(("groups", "rows"), "samples"),
        P(None, None, "rows", "samples"),
        P(None, "rows"),
        P(),
        P("groups", "samples"),
        P(None, None, "rows", None),
        P(None, "rows", None),
        P(None, None, "rows", None),
    )
    n = mesh.shape["rows"]

    def local(ancestor, panels, row_map, offsets, noise, inverse, inner_link, cross_link):
        args = (ancestor, panels, row_map, offsets, noise, inverse, inner_link, cross_link)
        fits = (
            mesh.shape["groups"] == 2
            and mesh.shape["samples"] == 4
            and n == 4
            and ancestor.shape[1] % (8 * n) == 0
            and inverse.shape[2] % 64 == 0
            and row_map.shape[1] % 8 == 0
        )
        return fused(n, *args) if fits else plain(*args)

    return jax.shard_map(
        local,
        mesh=mesh,
        in_specs=placed,
        out_specs=P(None, None, "rows", ("groups", "samples")),
        check_vma=False,
    )
```

```python
import functools

import jax
import jax.numpy as jnp
from jax import lax
from jax.experimental import pallas as pl
from jax.experimental.pallas import tpu as pltpu
from jax.sharding import PartitionSpec as P

F32 = jnp.float32
BF16 = jnp.bfloat16
NN = ((1,), (0,))
NT = ((1,), (1,))


def product(left, right):
    return jnp.dot(left, right, precision=lax.Precision.HIGHEST, preferred_element_type=F32)


def apply_inverse(target, partial_value, inverse_rows):
    rows_here = inverse_rows.shape[0]
    share = lax.psum_scatter(partial_value, "rows", scatter_dimension=0, tiled=True)
    first_own = lax.axis_index("rows") * rows_here
    residue = lax.dynamic_slice_in_dim(target, first_own, rows_here, 0) - share
    return product(inverse_rows, lax.all_gather(residue, "rows", axis=0, tiled=True))


def plain(ancestor, panels, row_map, offsets, noise, inverse, inner_link, cross_link):
    block_rows = inverse.shape[3]
    solved = [[None, None], [None, None]]
    for p in (1, 0):
        front_rows = jnp.take(ancestor, row_map[p], axis=0)
        window = lax.dynamic_slice_in_dim(noise, offsets[p], 2 * block_rows, 0)
        for b in (1, 0):
            whole = lax.all_gather(panels[p, b], "samples", axis=1, tiled=True)
            partial_value = product(whole.T, front_rows)
            if b == 0:
                partial_value = partial_value + product(inner_link[p].T, solved[p][1])
            if p == 0:
                for e in (0, 1):
                    partial_value = partial_value + product(cross_link[b, e].T, solved[1][e])
            target = window[b * block_rows : (b + 1) * block_rows]
            solved[p][b] = apply_inverse(target, partial_value, inverse[p, b])
    return jnp.stack([jnp.stack(solved[0]), jnp.stack(solved[1])])


def split(a):
    hi = a.astype(BF16)
    return hi, (a - hi.astype(F32)).astype(BF16)


def dot(a, b, dims):
    return lax.dot_general(a, b, (dims, ((), ())), preferred_element_type=F32)


def mm(a, b, dims):
    ah, al = split(a)
    bh, bl = b
    m = a.shape[0]
    both = dot(jnp.concatenate([ah, al], 0), bh, dims)
    return both[:m] + (both[m:] + dot(ah, bl, dims))


def kernel(
    n, rm_h, off_h, anc_h, pan_h, noise_h, inv_h, lnk_h, crs_h, out,
    rm, off, anc, nz, mats, mhi, mlo, pk, fr, tt, rsend, rrecv, osend, orecv,
    loc, ps, pr, zs, zr, b1s, b1r, b2s, b2r, b3s, b3r, rss, rsr, oss, osr,
):
    y = lax.axis_index("groups")
    z = lax.axis_index("rows")
    s = lax.axis_index("samples")
    x, c = s // 2, s % 2
    sx = (s + 2) % 4
    sib = s + 1 - 2 * c
    to_x, to_y, to_c = {"samples": sx}, {"groups": 1 - y}, {"samples": sib}
    block = mats.shape[3]
    share = mats.shape[2]
    piece = share // 8
    half = mats.shape[0] // 2
    w = rsend.shape[2]

    def remote(src, dst, ss, rs, where):
        return pltpu.make_async_remote_copy(
            src_ref=src, dst_ref=dst, send_sem=ss, recv_sem=rs,
            device_id=where, device_id_type=pl.DeviceIdType.MESH,
        )

    local = [
        pltpu.make_async_copy(pan_h.at[1], pk.at[1, :, s], loc.at[0]),
        pltpu.make_async_copy(pan_h.at[0], pk.at[0, :, s], loc.at[1]),
        pltpu.make_async_copy(inv_h, mats.at[0:4, z], loc.at[2]),
        pltpu.make_async_copy(lnk_h, mats.at[4:6, z], loc.at[3]),
        pltpu.make_async_copy(crs_h, mats.at[6:10, z], loc.at[4]),
        pltpu.make_async_copy(rm_h, rm, loc.at[5]),
        pltpu.make_async_copy(off_h, off, loc.at[6]),
        pltpu.make_async_copy(anc_h, anc, loc.at[7]),
        pltpu.make_async_copy(noise_h, nz, loc.at[8]),
    ]
    for copy in local:
        copy.start()

    barrier = pltpu.get_barrier_semaphore()
    peers = [{"rows": (z + k) % n} for k in range(1, n)] + [to_x, to_y, to_c]
    for peer in peers:
        pl.semaphore_signal(barrier, inc=1, device_id=peer, device_id_type=pl.DeviceIdType.MESH)

    for i in range(7):
        local[i].wait()

    pl.semaphore_wait(barrier, len(peers))

    pending = []

    def go(copy):
        copy.start()
        pending.append(copy)
        return copy

    pan_x, pan_c, pan_r = {}, {}, {}
    for p in (1, 0):
        ref = pk.at[p, :, s]
        pan_x[p] = go(remote(ref, ref, ps.at[p, 0], pr.at[p, 0], to_x))
        pan_c[p] = go(remote(ref, ref, ps.at[p, 1], pr.at[p, 1], to_c))

    def at_rows(q):
        return pl.ds(pl.multiple_of(q * piece, piece), piece)

    q = c * 4 + x * 2 + y
    qx = c * 4 + (1 - x) * 2 + y
    qy = c * 4 + x * 2 + (1 - y)
    sets = [(0, half), (half, 2 * half)]
    stage_z = {}
    for k in range(1, n):
        for g, (lo, hi) in enumerate(sets):
            ref = mats.at[lo:hi, z, at_rows(q)]
            stage_z[k, g] = go(remote(ref, ref, zs.at[k, g], zr.at[k, g], {"rows": (z + k) % n}))

    local[7].wait()
    for p in (1, 0):
        def rows8(i, carry, p=p):
            for r in range(8):
                fr[p, pl.ds(i * 8 + r, 1), :] = anc[pl.ds(rm[p, i * 8 + r], 1), :]
            return carry

        lax.fori_loop(0, fr.shape[1] // 8, rows8, 0)
    local[8].wait()
    for p in range(2):
        tt[p] = nz[pl.ds(off[p], 2 * block), :].T

    stage_1 = {}

    def forward(p):
        pan_x[p].wait_recv()
        ref = pk.at[p, :, sx]
        pan_r[p] = go(remote(ref, ref, ps.at[p, 2], pr.at[p, 2], to_c))

    def reduce(p):
        ft = fr[p].T
        pan_c[p].wait_recv()
        pan_r[p].wait_recv()
        whole = jnp.concatenate(
            [mm(ft, split(pk[p, b].reshape(block, ft.shape[1])), NT) for b in range(2)], axis=1
        )
        for j in range(n):
            rsend[j, p] = whole[j * w : (j + 1) * w]
        for k in range(1, n):
            go(remote(rsend.at[(z + k) % n, p], rrecv.at[k, p], rss.at[k, p], rsr.at[k, p], {"rows": (z + k) % n}))

    forward(1)
    reduce(1)
    forward(0)
    for k in range(1, n):
        zz = (z + n - k) % n
        for g, (lo, hi) in enumerate(sets):
            stage_z[k, g].wait_recv()
            ref = mats.at[lo:hi, zz, at_rows(q)]
            stage_1[k, g] = go(remote(ref, ref, b1s.at[k, g], b1r.at[k, g], (to_x, to_y)[g]))
    reduce(0)

    stage_2 = {}
    for k in range(1, n):
        zz = (z + n - k) % n
        for g, (lo, hi) in enumerate(sets):
            stage_1[k, g].wait_recv()
            for h, qq in enumerate((q, (qx, qy)[g])):
                ref = mats.at[lo:hi, zz, at_rows(qq)]
                stage_2[k, g, h] = go(remote(ref, ref, b2s.at[k, g, h], b2r.at[k, g, h], (to_y, to_x)[g]))
    stage_3 = {}
    for k in range(1, n):
        zz = (z + n - k) % n
        for g, (lo, hi) in enumerate(sets):
            stage_2[k, g, 0].wait_recv()
            stage_2[k, g, 1].wait_recv()
            ref = mats.at[lo:hi, zz, pl.ds(pl.multiple_of(c * 4 * piece, 4 * piece), 4 * piece)]
            stage_3[k, g] = go(remote(ref, ref, b3s.at[k, g], b3r.at[k, g], to_c))
    for k in range(1, n):
        for g in range(2):
            stage_3[k, g].wait_recv()

    for i in range(2 * half):
        mhi[i], mlo[i] = split(mats[i].reshape(block, block))

    def matrix(i):
        return mhi[i], mlo[i]

    def residue(p):
        total = rsend[z, p]
        for k in range(1, n):
            remote(rsend.at[(z + k) % n, p], rrecv.at[k, p], rss.at[k, p], rsr.at[k, p], {"rows": (z + k) % n}).wait_recv()
            total = total + rrecv[k, p]
        return tt[p, pl.ds(pl.multiple_of(z * w, w), w), :] - total

    def back(p, first, second):
        for i in range(n):
            cut = slice(i * share, (i + 1) * share)
            osend[p, i] = jnp.concatenate([first[:, cut], second[:, cut]], axis=1)
        orecv[p, z] = osend[p, z]
        for k in range(1, n):
            go(remote(osend.at[p, (z + k) % n], orecv.at[p, z], oss.at[k, p], osr.at[k, p], {"rows": (z + k) % n}))

    res = residue(1)
    s11 = mm(res[:, block:], matrix(3), NT)
    s10 = mm(res[:, :block] - mm(s11, matrix(5), NN), matrix(2), NT)
    back(1, s10, s11)
    res = residue(0)
    s01 = mm(res[:, block:] - mm(s10, matrix(8), NN) - mm(s11, matrix(9), NN), matrix(1), NT)
    s00 = mm(
        res[:, :block] - mm(s10, matrix(6), NN) - mm(s11, matrix(7), NN) - mm(s01, matrix(4), NN),
        matrix(0), NT,
    )
    back(0, s00, s01)

    for p in (1, 0):
        for k in range(1, n):
            src = (z + n - k) % n
            remote(osend.at[p, src], orecv.at[p, src], oss.at[k, p], osr.at[k, p], {"rows": src}).wait_recv()
        out[p] = orecv[p].reshape(n * w, 2 * share).T.reshape(2, share, n * w)

    for copy in pending:
        copy.wait_send()


def fused(n, ancestor, panels, row_map, offsets, noise, inverse, inner_link, cross_link):
    share, block = inverse.shape[2:]
    lanes = ancestor.shape[1]
    w = lanes // n
    dma = pltpu.SemaphoreType.DMA
    anyspace = pl.BlockSpec(memory_space=pl.ANY)
    return pl.pallas_call(
        functools.partial(kernel, n),
        name="substitute",
        out_shape=pltpu.VMEM((2, 2, share, lanes), F32),
        in_specs=[anyspace] * 8,
        out_specs=pl.BlockSpec(memory_space=pltpu.VMEM),
        scratch_shapes=[
            pltpu.SMEM(row_map.shape, jnp.int32),
            pltpu.SMEM(offsets.shape, jnp.int32),
            pltpu.VMEM(ancestor.shape, F32),
            pltpu.VMEM(noise.shape, F32),
            pltpu.VMEM((10, n, share, block), F32),
            pltpu.VMEM((10, block, block), BF16),
            pltpu.VMEM((10, block, block), BF16),
            pltpu.VMEM((2, 2, 4, panels.shape[3], panels.shape[2]), F32),
            pltpu.VMEM((2, row_map.shape[1], lanes), F32),
            pltpu.VMEM((2, lanes, 2 * block), F32),
            pltpu.VMEM((n, 2, w, 2 * block), F32),
            pltpu.VMEM((n, 2, w, 2 * block), F32),
            pltpu.VMEM((2, n, w, 2 * share), F32),
            pltpu.VMEM((2, n, w, 2 * share), F32),
            dma((9,)), dma((2, 3)), dma((2, 3)),
            dma((n, 2)), dma((n, 2)),
            dma((n, 2)), dma((n, 2)),
            dma((n, 2, 2)), dma((n, 2, 2)),
            dma((n, 2)), dma((n, 2)),
            dma((n, 2)), dma((n, 2)),
            dma((n, 2)), dma((n, 2)),
        ],
        compiler_params=pltpu.CompilerParams(collective_id=0, has_side_effects=True),
    )(
        row_map, offsets, ancestor, panels.swapaxes(2, 3), noise,
        inverse.reshape(4, share, block), inner_link, cross_link.reshape(4, share, block),
    )


def solution(mesh):
    placed = (
        P(("groups", "rows"), "samples"),
        P(None, None, "rows", "samples"),
        P(None, "rows"),
        P(),
        P("groups", "samples"),
        P(None, None, "rows", None),
        P(None, "rows", None),
        P(None, None, "rows", None),
    )
    n = mesh.shape["rows"]

    def local(ancestor, panels, row_map, offsets, noise, inverse, inner_link, cross_link):
        args = (ancestor, panels, row_map, offsets, noise, inverse, inner_link, cross_link)
        fits = (
            mesh.shape["groups"] == 2
            and mesh.shape["samples"] == 4
            and ancestor.shape[1] % (8 * n) == 0
            and inverse.shape[2] % 64 == 0
            and row_map.shape[1] % 8 == 0
        )
        return fused(n, *args) if fits else plain(*args)

    return jax.shard_map(
        local,
        mesh=mesh,
        in_specs=placed,
        out_specs=P(None, None, "rows", ("groups", "samples")),
        check_vma=False,
    )
```
